32 devices in a mesh: slab: 4 (over z), bulk: 8 (over y, x, core).
Axes of the slice: x: 2, y: 2, z: 4, core: 2. Of those that a mesh axis runs over, the one named last changes fastest.
Arguments:
- atom_counts: int32 [16, 64, 1024], P('slab', 'bulk'), may hold values from 0 to 15
- ion_flags: int32 [16, 64, 1024], P(None, 'bulk', 'slab'), may hold values 0 or 1
- charge_cells: int32 [32768], P(('slab', 'bulk')), may hold values from 0 to 32767
- charge_values: float32 [32768], P(('slab', 'bulk')), may hold values from -16 to 16
Outputs:
- potential: float32 [16, 64, 1024], P(None, 'bulk', 'slab')
- misfit: float32 [16, 64, 1024], P(None, 'bulk', 'slab')
The draws below stay inside these ranges and needn't reach their ends.
Inputs may be any that keep to these rules, and one draw needn't show every extreme that they name: Entry i of charge_cells is the flat index z * 8 * 256 + x * 256 + y of a cell in the brick of the device that holds entry i; cells may repeat.
All inputs are finite; a program needn't handle non-finite values. No bound on the sum of `ion_flags` on one device may be relied on, other than what follows from the above.
Results may differ from the reference program's by a relative error of at most 0.0001.
Values sent between devices are 32-bit elements; how exact they have to be, the bound alone decides.
A program may use at most 128 MiB of HBM per device.

```python
import math
import jax
import jax.numpy as jnp
import numpy as np
from jax import lax

CX = 8
CYB = 256
Q = 1024
GRID_LEVEL_COUNT = 4
SWEEPS = 1
COARSE = 8
NEWTON = 2
NZ = 16
NX = 64
NY = 1024
CHARGES = 32768
N_BULK = 8


def place_ends(array, stream_key, low, top_value):
    index_at = [jax.random.randint(jax.random.fold_in(stream_key, axis), (), 0, length) for axis, length in enumerate(array.shape)]
    main_axis = array.shape.index(max(array.shape))
    next_to = index_at[:main_axis] + [(index_at[main_axis] + 1) % array.shape[main_axis]] + index_at[main_axis + 1:]
    return array.at[tuple(index_at)].set(low).at[tuple(next_to)].set(top_value)


def block_scale(own_key, shape, cuts, low, high):
    def one(dim, parts):
        draws = jax.random.uniform(jax.random.fold_in(jax.random.fold_in(own_key, 6), dim), (parts,), jnp.float32, low / len(cuts), high / len(cuts))
        return jnp.repeat(jnp.exp(draws), shape[dim] // parts).reshape((-1,) + (1,) * (len(shape) - dim - 1))

    factor_of = one(*cuts[0])
    for cut in cuts[1:]:
        factor_of = factor_of * one(*cut)
    return factor_of


def rank_table(number_of, lean):
    loads = [(1 << 20) // math.isqrt(rank ** lean) + 1 for rank in range(1, number_of + 1)]
    spread = 1 + sum(loads) // (1 << 30)
    return np.cumsum(np.array([max(1, weight // spread) for weight in loads]))


def ranked_ids(own_key, shape, number_of, slope):
    listing = rank_table(number_of, slope)
    pick = jax.random.randint(jax.random.fold_in(own_key, 1), shape, 0, int(listing[number_of - 1]))
    standing = jnp.searchsorted(jnp.asarray(listing, jnp.int32), pick, side="right")
    return jax.random.permutation(jax.random.fold_in(own_key, 2), number_of)[standing].astype(jnp.int32)


def normal_values(key, dims, scale, bound, split=(), held_as=jnp.bfloat16):
    drawn = scale * jax.random.normal(key, dims, jnp.float32)
    if split:
        drawn = drawn * block_scale(key, dims, split, -0.22, 0.18)
    return jnp.clip(drawn, -bound, bound).astype(held_as)


def setup_inputs(seed: int = 0) -> dict:
    splits = jax.random.split(jax.random.key(seed), 5)
    return {
        "atom_counts": place_ends(ranked_ids(splits[0], (NZ, NX, NY), 16, 2), jax.random.fold_in(splits[0], 3), 0, 15).astype(jnp.int32),
        "ion_flags": place_ends((jax.random.randint(splits[1], (NZ, NX, NY), 0, 4) < 1).astype(jnp.int32), jax.random.fold_in(splits[1], 1), 0, 1),
        "charge_cells": place_ends(jax.random.randint(splits[2], (CHARGES,), 0, NZ * CX * CYB), jax.random.fold_in(splits[2], 1), 0, (NZ * CX * CYB) - 1).astype(jnp.int32),
        "charge_values": normal_values(splits[3], (CHARGES,), 4.0, 16.0, ((0, 32),), jnp.float32),
    }


taper_raw = np.exp(-0.5 * (np.arange(-4, 5) / 1.5) ** 2)
taper_weights = taper_raw / taper_raw.sum()
damping = 0.8
screening = 1.0
density_scale = 2.0


def taper_sum(padded, dimension):
    length = padded.shape[dimension] - 8
    summed = float(taper_weights[0]) * lax.slice_in_dim(padded, 0, length, axis=dimension)
    for offset in range(1, 9):
        summed = summed + float(taper_weights[offset]) * lax.slice_in_dim(padded, offset, offset + length, axis=dimension)
    return summed


def smooth_along(values_in, dimension):
    widths = [(0, 0), (0, 0), (0, 0)]
    widths[dimension] = (4, 4)
    return taper_sum(jnp.pad(values_in, widths), dimension)


def shifted(padded, dimension, offset):
    starts = [1, 1, 1]
    starts[dimension] = 1 + offset
    limits = [starts[0] + padded.shape[0] - 2, starts[1] + padded.shape[1] - 2, starts[2] + padded.shape[2] - 2]
    return lax.slice(padded, starts, limits)


def laplace_part(field_pad, dielectric_pad, scaling):
    middle = shifted(field_pad, 0, 0)
    dielectric_mid = shifted(dielectric_pad, 0, 0)
    summed = jnp.zeros_like(middle)
    for dimension in range(3):
        for offset in (-1, 1):
            weight_face = 0.5 * (dielectric_mid + shifted(dielectric_pad, dimension, offset))
            summed = summed + weight_face * (middle - shifted(field_pad, dimension, offset))
    return scaling * summed


def total_face_weight(dielectric_pad, scaling):
    dielectric_mid = shifted(dielectric_pad, 0, 0)
    summed = jnp.zeros_like(dielectric_mid)
    for dimension in range(3):
        for offset in (-1, 1):
            summed = summed + 0.5 * (dielectric_mid + shifted(dielectric_pad, dimension, offset))
    return scaling * summed


def coarsen(values_in):
    sizes_in = values_in.shape
    blocks = values_in.reshape(sizes_in[0] // 2, 2, sizes_in[1] // 2, 2, sizes_in[2] // 2, 2)
    return blocks.sum(axis=(1, 3, 5)) * 0.125


def refine(coarse):
    return jnp.repeat(jnp.repeat(jnp.repeat(coarse, 2, axis=0), 2, axis=1), 2, axis=2)


def multigrid(grid_height, target, level_list):
    dielectric_pad, reaction, diagonal, scaling = level_list[grid_height]

    def operate(iterate):
        return laplace_part(jnp.pad(iterate, 1), dielectric_pad, scaling) + reaction * iterate

    deepest = grid_height == len(level_list) - 1
    iterate = damping * target / diagonal
    repeats = COARSE - 1 if deepest else SWEEPS - 1
    for repeat in range(repeats):
        iterate = iterate + damping * (target - operate(iterate)) / diagonal
    if deepest:
        return iterate
    residue = target - operate(iterate)
    iterate = iterate + refine(multigrid(grid_height + 1, coarsen(residue), level_list))
    for repeat in range(SWEEPS):
        iterate = iterate + damping * (target - operate(iterate)) / diagonal
    return iterate


def reference(atom_counts, ion_flags, charge_cells, charge_values):
    density = atom_counts.astype(jnp.float32)
    smoothed = smooth_along(smooth_along(smooth_along(density, 2), 0), 1)
    shading = jnp.exp(-smoothed / density_scale)
    dielectric = 2.0 + 78.0 * shading
    reaction_base = screening * shading * shading * (1.0 - ion_flags.astype(jnp.float32))
    serial = jnp.arange(CHARGES, dtype=jnp.int32)
    device = serial // Q
    slab_index = device // N_BULK
    bulk_index = device % N_BULK
    planes = charge_cells // (CX * CYB)
    remainder = charge_cells % (CX * CYB)
    row_index = bulk_index * CX + remainder // CYB
    column = slab_index * CYB + remainder % CYB
    source = jnp.zeros((NZ, NX, NY), jnp.float32).at[planes, row_index, column].add(charge_values)
    dielectrics = [dielectric]
    for grid_height in range(1, GRID_LEVEL_COUNT):
        dielectrics.append(coarsen(dielectrics[-1]))
    scale_factors = [0.25 ** grid_height for grid_height in range(GRID_LEVEL_COUNT)]
    padded_dielectric_maps = [jnp.pad(item, 1) for item in dielectrics]
    summed_face_weights = [total_face_weight(padded_dielectric_maps[grid_height], scale_factors[grid_height]) for grid_height in range(GRID_LEVEL_COUNT)]
    potential = jnp.zeros((NZ, NX, NY), jnp.float32)
    for newton in range(NEWTON):
        misfit = laplace_part(jnp.pad(potential, 1), padded_dielectric_maps[0], 1.0) + reaction_base * jnp.sinh(potential) - source
        reaction_terms = [reaction_base * jnp.cosh(potential)]
        for grid_height in range(1, GRID_LEVEL_COUNT):
            reaction_terms.append(coarsen(reaction_terms[-1]))
        level_list = [(padded_dielectric_maps[grid_height], reaction_terms[grid_height], summed_face_weights[grid_height] + reaction_terms[grid_height], scale_factors[grid_height]) for grid_height in range(GRID_LEVEL_COUNT)]
        potential = potential + multigrid(0, -misfit, level_list)
    misfit = laplace_part(jnp.pad(potential, 1), padded_dielectric_maps[0], 1.0) + reaction_base * jnp.sinh(potential) - source
    return potential, misfit
```

```python
import jax
import jax.numpy as jnp
import numpy as np
from jax import lax
from jax.experimental import pallas as pl
from jax.experimental.pallas import tpu as pltpu
from jax.sharding import PartitionSpec as P

GRID_LEVEL_COUNT = 4
COARSE = 8
NEWTON = 2


taper_raw = np.exp(-0.5 * (np.arange(-4, 5) / 1.5) ** 2)
taper_weights = taper_raw / taper_raw.sum()
damping = 0.8
screening = 1.0
density_scale = 2.0


def padded_2(block, sides, width):
    for axis, dim in sides:
        count = lax.axis_size(axis)
        forward = [(i, i + 1) for i in range(count - 1)]
        backward = [(target, source) for source, target in forward]
        low = lax.ppermute(
            lax.slice_in_dim(block, block.shape[dim] - width, None, axis=dim), axis, forward
        )
        high = lax.ppermute(lax.slice_in_dim(block, 0, width, axis=dim), axis, backward)
        block = jnp.concatenate([low, block, high], axis=dim)
    return block


def taper_sum(padded, dimension):
    length = padded.shape[dimension] - 8
    summed = float(taper_weights[0]) * lax.slice_in_dim(padded, 0, length, axis=dimension)
    for offset in range(1, 9):
        summed = summed + float(taper_weights[offset]) * lax.slice_in_dim(
            padded, offset, offset + length, axis=dimension
        )
    return summed


MESH_ID = pl.DeviceIdType.MESH
LN2 = float(np.log(2.0))


def iota(shape, dim):
    return lax.broadcasted_iota(jnp.int32, shape, dim)


def log2(n):
    return int(n).bit_length() - 1


def mm(a, b):
    return lax.dot_general(
        a, b, (((1,), (0,)), ((), ())),
        precision=lax.Precision.HIGHEST, preferred_element_type=jnp.float32,
    )


def pick(shape, test, value):
    return jnp.where(test(iota(shape, 0), iota(shape, 1)), jnp.float32(value), jnp.float32(0.0))


def left_coarse(rows, z):
    lz = log2(z)

    def test(i, j):
        return ((i >> (lz - 1)) == (j >> (lz + 1))) & (
            (i & (z // 2 - 1)) == ((j & (z - 1)) >> 1)
        )

    return pick((rows // 4, rows), test, 0.25)


def left_fine(rows, z):
    lz = log2(z)

    def test(j, i):
        return ((i >> (lz - 1)) == (j >> (lz + 1))) & (
            (i & (z // 2 - 1)) == ((j & (z - 1)) >> 1)
        )

    return pick((rows, rows // 4), test, 1.0)


def right_coarse(y):
    return pick((y, y // 2), lambda i, j: (i >> 1) == j, 0.5)


def right_fine(y):
    return pick((y // 2, y), lambda i, j: i == (j >> 1), 1.0)


def coarse2(v, z):
    return mm(mm(left_coarse(v.shape[0], z), v), right_coarse(v.shape[1]))


def fine2(v, z):
    return mm(mm(left_fine(v.shape[0] * 4, z), v), right_fine(v.shape[1] * 2))


def neighbours(v, z, xlo, xhi, edge):
    rows, y = v.shape
    row, lane = iota(v.shape, 0), iota(v.shape, 1)
    if xlo is None:
        xm = jnp.where(row < z, 0.0, pltpu.roll(v, z, 0))
        xp = jnp.where(row >= rows - z, 0.0, pltpu.roll(v, rows - z, 0))
        edge = jnp.zeros_like(v)
    else:
        xm = jnp.concatenate([xlo, v[: rows - z]], axis=0)
        xp = jnp.concatenate([v[z:], xhi], axis=0)
    zrow = row & (z - 1)
    zm = jnp.where(zrow == 0, 0.0, pltpu.roll(v, 1, 0))
    zp = jnp.where(zrow == z - 1, 0.0, pltpu.roll(v, rows - 1, 0))
    ym = jnp.where(lane == 0, edge, pltpu.roll(v, 1, 1))
    yp = jnp.where(lane == y - 1, edge, pltpu.roll(v, y - 1, 1))
    return xm, xp, zm, zp, ym, yp


def put_weights(w_ref, d, z, halo, scaling):
    total = None
    for i, other in enumerate(neighbours(d, z, *halo)):
        w = (0.5 * scaling) * (d + other)
        w_ref[i] = w
        total = w if total is None else total + w
    return total


def laplace(w_ref, v, z, halo):
    total = None
    for i, other in enumerate(neighbours(v, z, *halo)):
        term = w_ref[i] * (v - other)
        total = term if total is None else total + term
    return total


NO_HALO = (None, None, None)


def sinh_cosh(p):
    a, b = jnp.exp(p - LN2), jnp.exp(-p - LN2)
    q = jnp.minimum(p * p, 1.0)
    small = p * (
        1.0
        + q * (1 / 6) * (1.0 + q * (1 / 20) * (1.0 + q * (1 / 42) * (1.0 + q * (1 / 72) * (1.0 + q * (1 / 110)))))
    )
    return jnp.where(jnp.abs(p) < 1.0, small, a - b), a + b


def solver(
    slabs, bulks, nz, cx, y,
    d_in, rb_in, src_in, pot_ref, mis_ref,
    w0, w1, w2, w3, v2_ref,
    sx0, hx0, sy0, hy0, sx1, hx1, sy1, hy1,
    own, buf1, buf2,
    send_sem, recv_sem, s1_send, s1_recv, s2_send, s2_recv,
):
    s, b = lax.axis_index("slab"), lax.axis_index("bulk")
    z0, z1, z2, z3 = nz, nz // 2, nz // 4, nz // 8
    rows0, rows1 = cx * z0, (cx // 2) * z1
    r2 = (cx // 4) * z2
    y1 = y // 2
    y2 = y // 4
    for ref in (hx0, hy0, hx1, hy1):
        ref[...] = jnp.zeros_like(ref)

    barrier = pltpu.get_barrier_semaphore()
    for k in range(1, slabs):
        pl.semaphore_signal(
            barrier, inc=1, device_id=(lax.rem(s + k, slabs), b), device_id_type=MESH_ID
        )
    for k in range(1, bulks):
        pl.semaphore_signal(
            barrier, inc=1, device_id=(s, lax.rem(b + k, bulks)), device_id_type=MESH_ID
        )
    pl.semaphore_wait(barrier, slabs + bulks - 2)

    def halo_copies(level, phase):
        sx, hx, sy, hy = (sx0, hx0, sy0, hy0) if level == 0 else (sx1, hx1, sy1, hy1)
        slot = phase if level == 0 else 7 + phase
        made = []
        for side, (src, dst, to, can_send, can_recv) in enumerate((
            (sx.at[phase, 0], hx.at[phase, 0], (s, b + 1), b < bulks - 1, b > 0),
            (sx.at[phase, 1], hx.at[phase, 1], (s, b - 1), b > 0, b < bulks - 1),
            (sy.at[phase, 0], hy.at[phase, 0], (s + 1, b), s < slabs - 1, s > 0),
            (sy.at[phase, 1], hy.at[phase, 1], (s - 1, b), s > 0, s < slabs - 1),
        )):
            copy = pltpu.make_async_remote_copy(
                src_ref=src, dst_ref=dst,
                send_sem=send_sem.at[slot, side], recv_sem=recv_sem.at[slot, side],
                device_id=to, device_id_type=MESH_ID,
            )
            made.append((copy, can_send, can_recv))
        return made

    def start(level, phase, v):
        sx, sy = (sx0, sy0) if level == 0 else (sx1, sy1)
        z = z0 if level == 0 else z1
        rows, ys = v.shape
        sx[phase, 0] = v[rows - z :]
        sx[phase, 1] = v[:z]
        lane = iota((8, 128), 1)
        for side, at in ((0, ys - 1), (1, 0)):
            packed = jnp.zeros((8, 128), jnp.float32)
            for k in range(rows // 8):
                column = jnp.broadcast_to(v[8 * k : 8 * k + 8, at : at + 1], (8, 128))
                packed = jnp.where(lane == k, column, packed)
            sy[phase, side] = packed
        for copy, can_send, _ in halo_copies(level, phase):
            pl.when(can_send)(copy.start)

    def finish(level, phase):
        hx, hy = (hx0, hy0) if level == 0 else (hx1, hy1)
        rows, ys = (rows0, y) if level == 0 else (rows1, y1)
        for copy, _, can_recv in halo_copies(level, phase):
            pl.when(can_recv)(copy.wait_recv)
        low, high = hy[phase, 0], hy[phase, 1]
        lane = iota((8, ys), 1)
        tiles = []
        for k in range(rows // 8):
            tiles.append(jnp.where(
                lane == 0,
                jnp.broadcast_to(low[:, k : k + 1], (8, ys)),
                jnp.broadcast_to(high[:, k : k + 1], (8, ys)),
            ))
        return hx[phase, 0], hx[phase, 1], jnp.concatenate(tiles, axis=0)

    def exchange(level, phase, v):
        start(level, phase, v)
        return finish(level, phase)

    def gather_copies(n, stage):
        made = []
        size, me = (slabs, s) if stage == 0 else (bulks, b)
        for k in range(1, size):
            to = lax.rem(me + k, size)
            came = lax.rem(me + size - k, size)
            if stage == 0:
                make = lambda slot: pltpu.make_async_remote_copy(
                    src_ref=own.at[n], dst_ref=buf1.at[n, slot],
                    send_sem=s1_send.at[n, k], recv_sem=s1_recv.at[n, k],
                    device_id=(to, b), device_id_type=MESH_ID,
                )
            else:
                make = lambda slot: pltpu.make_async_remote_copy(
                    src_ref=buf1.at[n], dst_ref=buf2.at[n, slot],
                    send_sem=s2_send.at[n, k], recv_sem=s2_recv.at[n, k],
                    device_id=(s, to), device_id_type=MESH_ID,
                )
            made.append((make(me), make(came)))
        return made

    def gather(n, message):
        own[n] = message
        for out, _ in gather_copies(n, 0):
            out.start()
        buf1[n, s] = message
        for _, into in gather_copies(n, 0):
            into.wait_recv()
        for out, _ in gather_copies(n, 1):
            out.start()
        buf2[n, b] = buf1[n]
        for _, into in gather_copies(n, 1):
            into.wait_recv()

    def take(n, first, half):
        lane = iota((bulks * r2, 128), 1)
        tiles = []
        for t in range(slabs // 2):
            lo = buf2[n, :, 2 * t, first : first + r2, :].reshape(bulks * r2, 128)
            hi = buf2[n, :, 2 * t + 1, first : first + r2, :].reshape(bulks * r2, 128)
            if half == 0:
                hi = pltpu.roll(hi, 64, 1)
            else:
                lo = pltpu.roll(lo, 64, 1)
            tiles.append(jnp.where(lane < 64, lo, hi))
        return jnp.concatenate(tiles, axis=1)

    left12 = left_coarse(rows1, z1)
    right12a = pick((y1, 128), lambda i, j: (i >> 1) == j, 0.5)
    right12b = pick((y1, 128), lambda i, j: (i >> 1) + 64 == j, 0.5)

    d0 = d_in[...]
    start(0, 0, d0)
    d1 = coarse2(d0, z0)
    start(1, 0, d1)
    face0 = put_weights(w0, d0, z0, finish(0, 0), 1.0)
    face1 = put_weights(w1, d1, z1, finish(1, 0), 0.25)
    face2 = face3 = None
    rb = rb_in[...]
    src = src_in[...]
    pot = None
    for n in range(NEWTON):
        if n == 0:
            target, c0 = src, rb
        else:
            sh, ch = sinh_cosh(pot)
            target = src - laplace(w0, pot, z0, exchange(0, 3 * n, pot)) - rb * sh
            c0 = rb * ch
        step0 = damping / (face0 + c0)
        v0 = step0 * target
        start(0, 3 * n + 1, v0)
        c1 = coarse2(c0, z0)
        step1 = damping / (face1 + c1)
        res0 = target - laplace(w0, v0, z0, finish(0, 3 * n + 1)) - c0 * v0
        t1 = coarse2(res0, z0)
        v1 = step1 * t1
        start(1, n + 1, v1)
        xlo1, xhi1, edge1 = finish(1, n + 1)
        res1 = t1 - laplace(w1, v1, z1, (xlo1, xhi1, edge1)) - c1 * v1
        message = mm(left12, mm(res1, right12a) + mm(c1, right12b))
        if n == 0:
            extra = mm(left12, mm(d1, right12a))
        else:
            extra = jnp.zeros_like(message)
        gather(n, jnp.concatenate([message, extra], axis=0))
        t2, c2 = take(n, 0, 0), take(n, 0, 1)
        if n == 0:
            d2 = take(n, r2, 0)
            d3 = coarse2(d2, z2)
            face2 = put_weights(w2, d2, z2, NO_HALO, 0.25**2)
            face3 = put_weights(w3, d3, z3, NO_HALO, 0.25**3)
        step2 = damping / (face2 + c2)
        v2 = step2 * t2
        res2 = t2 - laplace(w2, v2, z2, NO_HALO) - c2 * v2
        t3, c3 = coarse2(res2, z2), coarse2(c2, z2)
        step3 = damping / (face3 + c3)
        v3 = step3 * t3
        for repeat in range(COARSE - 1):
            v3 = v3 + step3 * (t3 - laplace(w3, v3, z3, NO_HALO) - c3 * v3)
        v2 = v2 + fine2(v3, z2)
        v2 = v2 + step2 * (t2 - laplace(w2, v2, z2, NO_HALO) - c2 * v2)
        v2_ref[0:r2] = jnp.zeros((r2, slabs * y2), jnp.float32)
        v2_ref[r2 : r2 + bulks * r2] = v2
        v2_ref[r2 + bulks * r2 :] = jnp.zeros((r2, slabs * y2), jnp.float32)
        near = v2_ref[pl.ds(pl.multiple_of(b * r2, 8), 3 * r2), :]
        mine = pick((slabs * y2, y1), lambda i, j: i == (j >> 1) + s * y2, 1.0)
        rims = pick(
            (slabs * y2, y1),
            lambda i, j: ((j == 0) & (i == s * y2 - 1)) | ((j == y1 - 1) & (i == s * y2 + y2)),
            1.0,
        )
        near_mine = mm(near, mine)
        up = left_fine(rows1, z1)
        v1 = v1 + mm(up, near_mine[r2 : 2 * r2])
        xlo1 = xlo1 + mm(up, near_mine[0:r2])[rows1 - z1 :]
        xhi1 = xhi1 + mm(up, near_mine[2 * r2 :])[:z1]
        edge1 = edge1 + mm(up, mm(near[r2 : 2 * r2], rims))
        v1 = v1 + step1 * (t1 - laplace(w1, v1, z1, (xlo1, xhi1, edge1)) - c1 * v1)
        v0 = v0 + fine2(v1, z0)
        halo = exchange(0, 3 * n + 2, v0)
        v0 = v0 + step0 * (target - laplace(w0, v0, z0, halo) - c0 * v0)
        pot = v0 if n == 0 else pot + v0
    pot_ref[...] = pot
    sh, _ = sinh_cosh(pot)
    mis_ref[...] = laplace(w0, pot, z0, exchange(0, 3 * NEWTON, pot)) + rb * sh - src

    for level, count in ((0, 7), (1, 3)):
        for phase in range(count):
            for copy, can_send, _ in halo_copies(level, phase):
                pl.when(can_send)(copy.wait_send)
    for n in range(NEWTON):
        for stage in range(2):
            for out, _ in gather_copies(n, stage):
                out.wait_send()


def per_device(atom_counts, ion_flags, charge_cells, charge_values):
    slabs, bulks = lax.axis_size("slab"), lax.axis_size("bulk")
    density = atom_counts.astype(jnp.float32)
    along_y = taper_sum(jnp.pad(density, ((0, 0), (0, 0), (4, 4))), 2)
    extended = padded_2(along_y, (("slab", 0), ("bulk", 1)), 4)
    slab_shading = jnp.exp(-taper_sum(taper_sum(extended, 0), 1) / density_scale)
    shading = lax.all_to_all(slab_shading, "slab", split_axis=2, concat_axis=0, tiled=True)
    dielectric = 2.0 + 78.0 * shading
    access = shading * shading
    reaction_base = screening * access * (1.0 - ion_flags.astype(jnp.float32))
    flat_source = jnp.zeros((dielectric.size,), jnp.float32).at[charge_cells].add(charge_values)
    source = flat_source.reshape(dielectric.shape)

    nz, cx, y = dielectric.shape
    rows = nz * cx
    rows2 = (cx // 4) * (nz // 4)

    def flat(a):
        return a.transpose(1, 0, 2).reshape(rows, y)

    def back(a):
        return a.reshape(cx, nz, y).transpose(1, 0, 2)

    f32 = jnp.float32
    whole2 = (bulks * rows2, slabs * (y // 4))
    vm = pltpu.VMEM
    pot, mis = pl.pallas_call(
        lambda *refs: solver(slabs, bulks, nz, cx, y, *refs),
        out_shape=[jax.ShapeDtypeStruct((rows, y), f32)] * 2,
        in_specs=[pl.BlockSpec(memory_space=pltpu.VMEM)] * 3,
        out_specs=[pl.BlockSpec(memory_space=pltpu.VMEM)] * 2,
        scratch_shapes=[
            vm((6, rows, y), f32),
            vm((6, rows // 4, y // 2), f32),
            vm((6,) + whole2, f32),
            vm((6, whole2[0] // 4, whole2[1] // 2), f32),
            vm((whole2[0] + 2 * rows2, whole2[1]), f32),
            vm((7, 2, nz, y), f32), vm((7, 2, nz, y), f32),
            vm((7, 2, 8, 128), f32), vm((7, 2, 8, 128), f32),
            vm((3, 2, nz // 2, y // 2), f32), vm((3, 2, nz // 2, y // 2), f32),
            vm((3, 2, 8, 128), f32), vm((3, 2, 8, 128), f32),
            vm((2, 2 * rows2, 128), f32),
            vm((2, slabs, 2 * rows2, 128), f32),
            vm((2, bulks, slabs, 2 * rows2, 128), f32),
            pltpu.SemaphoreType.DMA((10, 4)), pltpu.SemaphoreType.DMA((10, 4)),
            pltpu.SemaphoreType.DMA((2, slabs)), pltpu.SemaphoreType.DMA((2, slabs)),
            pltpu.SemaphoreType.DMA((2, bulks)), pltpu.SemaphoreType.DMA((2, bulks)),
        ],
        compiler_params=pltpu.CompilerParams(
            collective_id=0, has_side_effects=True, vmem_limit_bytes=40 << 20
        ),
    )(flat(dielectric), flat(reaction_base), flat(source))
    return back(pot), back(mis)


def solution(mesh):
    placed = (
        P("slab", "bulk", None),
        P(None, "bulk", "slab"),
        P(("slab", "bulk")),
        P(("slab", "bulk")),
    )
    return jax.shard_map(
        per_device,
        mesh=mesh,
        in_specs=placed,
        out_specs=(P(None, "bulk", "slab"), P(None, "bulk", "slab")),
        check_vma=False,
    )
```

```python
import jax
import jax.numpy as jnp
import numpy as np
from jax import lax
from jax.experimental import pallas as pl
from jax.experimental.pallas import tpu as pltpu
from jax.sharding import PartitionSpec as P

GRID_LEVEL_COUNT = 4
COARSE = 8
NEWTON = 2


taper_raw = np.exp(-0.5 * (np.arange(-4, 5) / 1.5) ** 2)
taper_weights = taper_raw / taper_raw.sum()
damping = 0.8
screening = 1.0
density_scale = 2.0


MESH_ID = pl.DeviceIdType.MESH
LN2 = float(np.log(2.0))


def iota(shape, dim):
    return lax.broadcasted_iota(jnp.int32, shape, dim)


def log2(n):
    return int(n).bit_length() - 1


def mm(a, b):
    return lax.dot_general(
        a, b, (((1,), (0,)), ((), ())),
        precision=lax.Precision.HIGHEST, preferred_element_type=jnp.float32,
    )


def pick(shape, test, value):
    return jnp.where(test(iota(shape, 0), iota(shape, 1)), jnp.float32(value), jnp.float32(0.0))


def left_coarse(rows, z):
    lz = log2(z)

    def test(i, j):
        return ((i >> (lz - 1)) == (j >> (lz + 1))) & (
            (i & (z // 2 - 1)) == ((j & (z - 1)) >> 1)
        )

    return pick((rows // 4, rows), test, 0.25)


def left_fine(rows, z):
    lz = log2(z)

    def test(j, i):
        return ((i >> (lz - 1)) == (j >> (lz + 1))) & (
            (i & (z // 2 - 1)) == ((j & (z - 1)) >> 1)
        )

    return pick((rows, rows // 4), test, 1.0)


def right_coarse(y):
    return pick((y, y // 2), lambda i, j: (i >> 1) == j, 0.5)


def right_fine(y):
    return pick((y // 2, y), lambda i, j: i == (j >> 1), 1.0)


def coarse2(v, z):
    return mm(mm(left_coarse(v.shape[0], z), v), right_coarse(v.shape[1]))


def fine2(v, z):
    return mm(mm(left_fine(v.shape[0] * 4, z), v), right_fine(v.shape[1] * 2))


def neighbours(v, z, xlo, xhi, edge):
    rows, y = v.shape
    row, lane = iota(v.shape, 0), iota(v.shape, 1)
    if xlo is None:
        xm = jnp.where(row < z, 0.0, pltpu.roll(v, z, 0))
        xp = jnp.where(row >= rows - z, 0.0, pltpu.roll(v, rows - z, 0))
        edge = jnp.zeros_like(v)
    else:
        xm = jnp.concatenate([xlo, v[: rows - z]], axis=0)
        xp = jnp.concatenate([v[z:], xhi], axis=0)
    zrow = row & (z - 1)
    zm = jnp.where(zrow == 0, 0.0, pltpu.roll(v, 1, 0))
    zp = jnp.where(zrow == z - 1, 0.0, pltpu.roll(v, rows - 1, 0))
    ym = jnp.where(lane == 0, edge, pltpu.roll(v, 1, 1))
    yp = jnp.where(lane == y - 1, edge, pltpu.roll(v, y - 1, 1))
    return xm, xp, zm, zp, ym, yp


def put_weights(w_ref, d, z, halo, scaling):
    total = None
    for i, other in enumerate(neighbours(d, z, *halo)):
        w = (0.5 * scaling) * (d + other)
        w_ref[i] = w
        total = w if total is None else total + w
    return total


def laplace(w_ref, v, z, halo):
    total = None
    for i, other in enumerate(neighbours(v, z, *halo)):
        term = w_ref[i] * (v - other)
        total = term if total is None else total + term
    return total


NO_HALO = (None, None, None)


def sinh_cosh(p):
    a, b = jnp.exp(p - LN2), jnp.exp(-p - LN2)
    q = jnp.minimum(p * p, 1.0)
    small = p * (
        1.0
        + q * (1 / 6) * (1.0 + q * (1 / 20) * (1.0 + q * (1 / 42) * (1.0 + q * (1 / 72) * (1.0 + q * (1 / 110)))))
    )
    return jnp.where(jnp.abs(p) < 1.0, small, a - b), a + b


def taper_y(density):
    width = density.shape[1]
    lane = iota(density.shape, 1)
    summed = float(taper_weights[4]) * density
    for k in range(1, 5):
        before = jnp.where(lane < k, 0.0, pltpu.roll(density, k, 1))
        after = jnp.where(lane >= width - k, 0.0, pltpu.roll(density, width - k, 1))
        summed = summed + float(taper_weights[4 + k]) * (before + after)
    return summed


def taper_z(rows, z, cx):
    i, j = iota((rows, rows), 0), iota((rows, rows), 1)
    far = jnp.abs((i & (z - 1)) - (j >> log2(cx)))
    band = jnp.zeros((rows, rows), jnp.float32)
    for k in range(5):
        band = jnp.where(far == k, float(taper_weights[4 + k]), band)
    return jnp.where((i >> log2(z)) == (j & (cx - 1)), band, 0.0)


def scattered(cells, values, rows, z, cx, y):
    entries = cells.shape[1]
    ly, lx = log2(y), log2(cx)
    row = ((cells >> ly) & (cx - 1)) * z + (cells >> (ly + lx))
    at_row = jnp.where(iota((rows, entries), 0) == row, values, 0.0)
    at_y = jnp.where(iota((y, entries), 0) == (cells & (y - 1)), jnp.float32(1.0), jnp.float32(0.0))
    return lax.dot_general(
        at_row, at_y, (((1,), (1,)), ((), ())),
        precision=lax.Precision.HIGHEST, preferred_element_type=jnp.float32,
    )


def solver(
    slabs, bulks, nz, cx, y,
    atoms_in, flags_in, cells_in, values_in, pot_ref, mis_ref,
    ay, abuf, ty, hty,
    w0, w1, w2, w3, v2_ref,
    sx0, hx0, sy0, hy0, sx1, hx1, sy1, hy1,
    own, buf1, buf2,
    send_sem, recv_sem, s1_send, s1_recv, s2_send, s2_recv,
    a_send, a_recv, t_send, t_recv,
):
    s, b = lax.axis_index("slab"), lax.axis_index("bulk")
    z0, z1, z2, z3 = nz, nz // 2, nz // 4, nz // 8
    rows0, rows1 = cx * z0, (cx // 2) * z1
    r2 = (cx // 4) * z2
    y1 = y // 2
    y2 = y // 4
    for ref in (hx0, hy0, hx1, hy1, hty):
        ref[...] = jnp.zeros_like(ref)

    barrier = pltpu.get_barrier_semaphore()
    for k in range(1, slabs):
        pl.semaphore_signal(
            barrier, inc=1, device_id=(lax.rem(s + k, slabs), b), device_id_type=MESH_ID
        )
    for k in range(1, bulks):
        pl.semaphore_signal(
            barrier, inc=1, device_id=(s, lax.rem(b + k, bulks)), device_id_type=MESH_ID
        )
    pl.semaphore_wait(barrier, slabs + bulks - 2)

    def halo_copies(level, phase):
        sx, hx, sy, hy = (sx0, hx0, sy0, hy0) if level == 0 else (sx1, hx1, sy1, hy1)
        slot = phase if level == 0 else 7 + phase
        made = []
        for side, (src, dst, to, can_send, can_recv) in enumerate((
            (sx.at[phase, 0], hx.at[phase, 0], (s, b + 1), b < bulks - 1, b > 0),
            (sx.at[phase, 1], hx.at[phase, 1], (s, b - 1), b > 0, b < bulks - 1),
            (sy.at[phase, 0], hy.at[phase, 0], (s + 1, b), s < slabs - 1, s > 0),
            (sy.at[phase, 1], hy.at[phase, 1], (s - 1, b), s > 0, s < slabs - 1),
        )):
            copy = pltpu.make_async_remote_copy(
                src_ref=src, dst_ref=dst,
                send_sem=send_sem.at[slot, side], recv_sem=recv_sem.at[slot, side],
                device_id=to, device_id_type=MESH_ID,
            )
            made.append((copy, can_send, can_recv))
        return made

    def start(level, phase, v):
        sx, sy = (sx0, sy0) if level == 0 else (sx1, sy1)
        z = z0 if level == 0 else z1
        rows, ys = v.shape
        sx[phase, 0] = v[rows - z :]
        sx[phase, 1] = v[:z]
        lane = iota((8, 128), 1)
        for side, at in ((0, ys - 1), (1, 0)):
            packed = jnp.zeros((8, 128), jnp.float32)
            for k in range(rows // 8):
                column = jnp.broadcast_to(v[8 * k : 8 * k + 8, at : at + 1], (8, 128))
                packed = jnp.where(lane == k, column, packed)
            sy[phase, side] = packed
        for copy, can_send, _ in halo_copies(level, phase):
            pl.when(can_send)(copy.start)

    def finish(level, phase):
        hx, hy = (hx0, hy0) if level == 0 else (hx1, hy1)
        rows, ys = (rows0, y) if level == 0 else (rows1, y1)
        for copy, _, can_recv in halo_copies(level, phase):
            pl.when(can_recv)(copy.wait_recv)
        low, high = hy[phase, 0], hy[phase, 1]
        lane = iota((8, ys), 1)
        tiles = []
        for k in range(rows // 8):
            tiles.append(jnp.where(
                lane == 0,
                jnp.broadcast_to(low[:, k : k + 1], (8, ys)),
                jnp.broadcast_to(high[:, k : k + 1], (8, ys)),
            ))
        return hx[phase, 0], hx[phase, 1], jnp.concatenate(tiles, axis=0)

    def exchange(level, phase, v):
        start(level, phase, v)
        return finish(level, phase)

    def gather_copies(n, stage):
        made = []
        size, me = (slabs, s) if stage == 0 else (bulks, b)
        for k in range(1, size):
            to = lax.rem(me + k, size)
            came = lax.rem(me + size - k, size)
            if stage == 0:
                make = lambda slot: pltpu.make_async_remote_copy(
                    src_ref=own.at[n], dst_ref=buf1.at[n, slot],
                    send_sem=s1_send.at[n, k], recv_sem=s1_recv.at[n, k],
                    device_id=(to, b), device_id_type=MESH_ID,
                )
            else:
                make = lambda slot: pltpu.make_async_remote_copy(
                    src_ref=buf1.at[n], dst_ref=buf2.at[n, slot],
                    send_sem=s2_send.at[n, k], recv_sem=s2_recv.at[n, k],
                    device_id=(s, to), device_id_type=MESH_ID,
                )
            made.append((make(me), make(came)))
        return made

    def gather(n, message):
        own[n] = message
        for out, _ in gather_copies(n, 0):
            out.start()
        buf1[n, s] = message
        for _, into in gather_copies(n, 0):
            into.wait_recv()
        for out, _ in gather_copies(n, 1):
            out.start()
        buf2[n, b] = buf1[n]
        for _, into in gather_copies(n, 1):
            into.wait_recv()

    def take(n, first, half):
        lane = iota((bulks * r2, 128), 1)
        tiles = []
        for t in range(slabs // 2):
            lo = buf2[n, :, 2 * t, first : first + r2, :].reshape(bulks * r2, 128)
            hi = buf2[n, :, 2 * t + 1, first : first + r2, :].reshape(bulks * r2, 128)
            if half == 0:
                hi = pltpu.roll(hi, 64, 1)
            else:
                lo = pltpu.roll(lo, 64, 1)
            tiles.append(jnp.where(lane < 64, lo, hi))
        return jnp.concatenate(tiles, axis=1)

    left12 = left_coarse(rows1, z1)
    right12a = pick((y1, 128), lambda i, j: (i >> 1) == j, 0.5)
    right12b = pick((y1, 128), lambda i, j: (i >> 1) + 64 == j, 0.5)

    density = atoms_in[...].astype(jnp.float32).reshape(-1, slabs * y)
    smooth_y = taper_y(density)
    for t in range(slabs):
        ay[t] = smooth_y[:, t * y : (t + 1) * y]
    slab_copies = []
    for k in range(1, slabs):
        to, came = lax.rem(s + k, slabs), lax.rem(s + slabs - k, slabs)
        slab_copies.append([
            pltpu.make_async_remote_copy(
                src_ref=ay.at[to], dst_ref=abuf.at[slot],
                send_sem=a_send.at[k], recv_sem=a_recv.at[k],
                device_id=(to, b), device_id_type=MESH_ID,
            )
            for slot in (s, came)
        ])
    for out, _ in slab_copies:
        out.start()
    abuf[s] = ay[s]
    src = scattered(cells_in[...], values_in[...], rows0, z0, cx, y)
    to_x = pick((rows0, rows0), lambda i, j: (i >> log2(z0)) + ((i & (z0 - 1)) << log2(cx)) == j, 1.0)
    open_cells = 1.0 - mm(to_x, flags_in[...].astype(jnp.float32).reshape(rows0, y))
    along_z = taper_z(rows0, z0, cx)
    for _, into in slab_copies:
        into.wait_recv()
    smooth_z = mm(along_z, abuf[...].reshape(rows0, y))
    ty[0] = smooth_z[rows0 - 4 * z0 :]
    ty[1] = smooth_z[: 4 * z0]
    row_copies = []
    for side, (to, can_send, can_recv) in enumerate((
        ((s, b + 1), b < bulks - 1, b > 0),
        ((s, b - 1), b > 0, b < bulks - 1),
    )):
        row_copies.append((
            pltpu.make_async_remote_copy(
                src_ref=ty.at[side], dst_ref=hty.at[side],
                send_sem=t_send.at[side], recv_sem=t_recv.at[side],
                device_id=to, device_id_type=MESH_ID,
            ), can_send, can_recv,
        ))
    for copy, can_send, _ in row_copies:
        pl.when(can_send)(copy.start)
    for copy, _, can_recv in row_copies:
        pl.when(can_recv)(copy.wait_recv)
    extended = jnp.concatenate([hty[0], smooth_z, hty[1]], axis=0)
    smoothed = float(taper_weights[0]) * extended[:rows0]
    for k in range(1, 9):
        smoothed = smoothed + float(taper_weights[k]) * extended[k * z0 : k * z0 + rows0]
    shading = jnp.exp(-smoothed / density_scale)
    d0 = 2.0 + 78.0 * shading
    rb = screening * shading * shading * open_cells
    start(0, 0, d0)
    d1 = coarse2(d0, z0)
    start(1, 0, d1)
    face0 = put_weights(w0, d0, z0, finish(0, 0), 1.0)
    face1 = put_weights(w1, d1, z1, finish(1, 0), 0.25)
    face2 = face3 = None
    pot = None
    for n in range(NEWTON):
        if n == 0:
            target, c0 = src, rb
        else:
            sh, ch = sinh_cosh(pot)
            target = src - laplace(w0, pot, z0, exchange(0, 3 * n, pot)) - rb * sh
            c0 = rb * ch
        step0 = damping / (face0 + c0)
        v0 = step0 * target
        start(0, 3 * n + 1, v0)
        c1 = coarse2(c0, z0)
        step1 = damping / (face1 + c1)
        res0 = target - laplace(w0, v0, z0, finish(0, 3 * n + 1)) - c0 * v0
        t1 = coarse2(res0, z0)
        v1 = step1 * t1
        start(1, n + 1, v1)
        xlo1, xhi1, edge1 = finish(1, n + 1)
        res1 = t1 - laplace(w1, v1, z1, (xlo1, xhi1, edge1)) - c1 * v1
        message = mm(left12, mm(res1, right12a) + mm(c1, right12b))
        if n == 0:
            extra = mm(left12, mm(d1, right12a))
        else:
            extra = jnp.zeros_like(message)
        gather(n, jnp.concatenate([message, extra], axis=0))
        t2, c2 = take(n, 0, 0), take(n, 0, 1)
        if n == 0:
            d2 = take(n, r2, 0)
            d3 = coarse2(d2, z2)
            face2 = put_weights(w2, d2, z2, NO_HALO, 0.25**2)
            face3 = put_weights(w3, d3, z3, NO_HALO, 0.25**3)
        step2 = damping / (face2 + c2)
        v2 = step2 * t2
        res2 = t2 - laplace(w2, v2, z2, NO_HALO) - c2 * v2
        t3, c3 = coarse2(res2, z2), coarse2(c2, z2)
        step3 = damping / (face3 + c3)
        v3 = step3 * t3
        for repeat in range(COARSE - 1):
            v3 = v3 + step3 * (t3 - laplace(w3, v3, z3, NO_HALO) - c3 * v3)
        v2 = v2 + fine2(v3, z2)
        v2 = v2 + step2 * (t2 - laplace(w2, v2, z2, NO_HALO) - c2 * v2)
        v2_ref[0:r2] = jnp.zeros((r2, slabs * y2), jnp.float32)
        v2_ref[r2 : r2 + bulks * r2] = v2
        v2_ref[r2 + bulks * r2 :] = jnp.zeros((r2, slabs * y2), jnp.float32)
        near = v2_ref[pl.ds(pl.multiple_of(b * r2, 8), 3 * r2), :]
        mine = pick((slabs * y2, y1), lambda i, j: i == (j >> 1) + s * y2, 1.0)
        rims = pick(
            (slabs * y2, y1),
            lambda i, j: ((j == 0) & (i == s * y2 - 1)) | ((j == y1 - 1) & (i == s * y2 + y2)),
            1.0,
        )
        near_mine = mm(near, mine)
        up = left_fine(rows1, z1)
        v1 = v1 + mm(up, near_mine[r2 : 2 * r2])
        xlo1 = xlo1 + mm(up, near_mine[0:r2])[rows1 - z1 :]
        xhi1 = xhi1 + mm(up, near_mine[2 * r2 :])[:z1]
        edge1 = edge1 + mm(up, mm(near[r2 : 2 * r2], rims))
        v1 = v1 + step1 * (t1 - laplace(w1, v1, z1, (xlo1, xhi1, edge1)) - c1 * v1)
        v0 = v0 + fine2(v1, z0)
        halo = exchange(0, 3 * n + 2, v0)
        v0 = v0 + step0 * (target - laplace(w0, v0, z0, halo) - c0 * v0)
        pot = v0 if n == 0 else pot + v0
    start(0, 3 * NEWTON, pot)
    from_x = pick((rows0, rows0), lambda i, j: (j >> log2(z0)) + ((j & (z0 - 1)) << log2(cx)) == i, 1.0)
    pot_ref[...] = mm(from_x, pot).reshape(nz, cx, y)
    sh, _ = sinh_cosh(pot)
    misfit = laplace(w0, pot, z0, finish(0, 3 * NEWTON)) + rb * sh - src
    mis_ref[...] = mm(from_x, misfit).reshape(nz, cx, y)

    for out, _ in slab_copies:
        out.wait_send()
    for copy, can_send, _ in row_copies:
        pl.when(can_send)(copy.wait_send)
    for level, count in ((0, 7), (1, 3)):
        for phase in range(count):
            for copy, can_send, _ in halo_copies(level, phase):
                pl.when(can_send)(copy.wait_send)
    for n in range(NEWTON):
        for stage in range(2):
            for out, _ in gather_copies(n, stage):
                out.wait_send()


def per_device(atom_counts, ion_flags, charge_cells, charge_values):
    slabs, bulks = lax.axis_size("slab"), lax.axis_size("bulk")
    nz, cx, y = ion_flags.shape
    rows = nz * cx
    rows2 = (cx // 4) * (nz // 4)
    f32 = jnp.float32
    whole2 = (bulks * rows2, slabs * (y // 4))
    vm = pltpu.VMEM
    pot, mis = pl.pallas_call(
        lambda *refs: solver(slabs, bulks, nz, cx, y, *refs),
        out_shape=[jax.ShapeDtypeStruct((nz, cx, y), f32)] * 2,
        in_specs=[pl.BlockSpec(memory_space=pltpu.VMEM)] * 4,
        out_specs=[pl.BlockSpec(memory_space=pltpu.VMEM)] * 2,
        scratch_shapes=[
            vm((slabs, rows // slabs, y), f32), vm((slabs, rows // slabs, y), f32),
            vm((2, 4 * nz, y), f32), vm((2, 4 * nz, y), f32),
            vm((6, rows, y), f32),
            vm((6, rows // 4, y // 2), f32),
            vm((6,) + whole2, f32),
            vm((6, whole2[0] // 4, whole2[1] // 2), f32),
            vm((whole2[0] + 2 * rows2, whole2[1]), f32),
            vm((7, 2, nz, y), f32), vm((7, 2, nz, y), f32),
            vm((7, 2, 8, 128), f32), vm((7, 2, 8, 128), f32),
            vm((3, 2, nz // 2, y // 2), f32), vm((3, 2, nz // 2, y // 2), f32),
            vm((3, 2, 8, 128), f32), vm((3, 2, 8, 128), f32),
            vm((2, 2 * rows2, 128), f32),
            vm((2, slabs, 2 * rows2, 128), f32),
            vm((2, bulks, slabs, 2 * rows2, 128), f32),
            pltpu.SemaphoreType.DMA((10, 4)), pltpu.SemaphoreType.DMA((10, 4)),
            pltpu.SemaphoreType.DMA((2, slabs)), pltpu.SemaphoreType.DMA((2, slabs)),
            pltpu.SemaphoreType.DMA((2, bulks)), pltpu.SemaphoreType.DMA((2, bulks)),
            pltpu.SemaphoreType.DMA((slabs,)), pltpu.SemaphoreType.DMA((slabs,)),
            pltpu.SemaphoreType.DMA((2,)), pltpu.SemaphoreType.DMA((2,)),
        ],
        compiler_params=pltpu.CompilerParams(
            collective_id=0, has_side_effects=True, vmem_limit_bytes=40 << 20
        ),
    )(atom_counts, ion_flags, charge_cells[None], charge_values[None])
    return pot, mis


def solution(mesh):
    placed = (
        P("slab", "bulk", None),
        P(None, "bulk", "slab"),
        P(("slab", "bulk")),
        P(("slab", "bulk")),
    )
    return jax.shard_map(
        per_device,
        mesh=mesh,
        in_specs=placed,
        out_specs=(P(None, "bulk", "slab"), P(None, "bulk", "slab")),
        check_vma=False,
    )
```

```python
import jax
import jax.numpy as jnp
import numpy as np
from jax import lax
from jax.experimental import pallas as pl
from jax.experimental.pallas import tpu as pltpu
from jax.sharding import PartitionSpec as P

GRID_LEVEL_COUNT = 4
COARSE = 8
NEWTON = 2


taper_raw = np.exp(-0.5 * (np.arange(-4, 5) / 1.5) ** 2)
taper_weights = taper_raw / taper_raw.sum()
damping = 0.8
screening = 1.0
density_scale = 2.0


MESH_ID = pl.DeviceIdType.MESH
GATHER_UNROLL = 1
LN2 = float(np.log(2.0))


def iota(shape, dim):
    return lax.broadcasted_iota(jnp.int32, shape, dim)


def log2(n):
    return int(n).bit_length() - 1


def mm(a, b):
    return lax.dot_general(
        a, b, (((1,), (0,)), ((), ())),
        precision=lax.Precision.HIGHEST, preferred_element_type=jnp.float32,
    )


def pick(shape, test, value):
    return jnp.where(test(iota(shape, 0), iota(shape, 1)), jnp.float32(value), jnp.float32(0.0))


def left_coarse(rows, z):
    lz = log2(z)

    def test(i, j):
        return ((i >> (lz - 1)) == (j >> (lz + 1))) & (
            (i & (z // 2 - 1)) == ((j & (z - 1)) >> 1)
        )

    return pick((rows // 4, rows), test, 0.25)


def left_fine(rows, z):
    lz = log2(z)

    def test(j, i):
        return ((i >> (lz - 1)) == (j >> (lz + 1))) & (
            (i & (z // 2 - 1)) == ((j & (z - 1)) >> 1)
        )

    return pick((rows, rows // 4), test, 1.0)


def right_coarse(y):
    return pick((y, y // 2), lambda i, j: (i >> 1) == j, 0.5)


def right_fine(y):
    return pick((y // 2, y), lambda i, j: i == (j >> 1), 1.0)


def coarse2(v, z):
    return mm(mm(left_coarse(v.shape[0], z), v), right_coarse(v.shape[1]))


def fine2(v, z):
    return mm(mm(left_fine(v.shape[0] * 4, z), v), right_fine(v.shape[1] * 2))


def neighbours(v, z, xlo, xhi, edge):
    rows, y = v.shape
    row, lane = iota(v.shape, 0), iota(v.shape, 1)
    if xlo is None:
        xm = jnp.where(row < z, 0.0, pltpu.roll(v, z, 0))
        xp = jnp.where(row >= rows - z, 0.0, pltpu.roll(v, rows - z, 0))
        edge = jnp.zeros_like(v)
    else:
        xm = jnp.concatenate([xlo, v[: rows - z]], axis=0)
        xp = jnp.concatenate([v[z:], xhi], axis=0)
    zrow = row & (z - 1)
    zm = jnp.where(zrow == 0, 0.0, pltpu.roll(v, 1, 0))
    zp = jnp.where(zrow == z - 1, 0.0, pltpu.roll(v, rows - 1, 0))
    ym = jnp.where(lane == 0, edge, pltpu.roll(v, 1, 1))
    yp = jnp.where(lane == y - 1, edge, pltpu.roll(v, y - 1, 1))
    return xm, xp, zm, zp, ym, yp


def put_weights(w_ref, d, z, halo, scaling):
    total = None
    for i, other in enumerate(neighbours(d, z, *halo)):
        w = (0.5 * scaling) * (d + other)
        w_ref[i] = w
        total = w if total is None else total + w
    return total


def laplace(w_ref, v, z, halo):
    total = None
    for i, other in enumerate(neighbours(v, z, *halo)):
        term = w_ref[i] * (v - other)
        total = term if total is None else total + term
    return total


NO_HALO = (None, None, None)


def rim_part(w_ref, inner, z, halo):
    xlo, xhi, edge = halo
    rows, y = inner.shape
    lane = iota(inner.shape, 1)
    inner = inner - jnp.where(lane == 0, w_ref[4] * edge, jnp.where(lane == y - 1, w_ref[5] * edge, 0.0))
    first = inner[:z] - w_ref[0, :z] * xlo
    last = inner[rows - z :] - w_ref[1, rows - z :] * xhi
    return jnp.concatenate([first, inner[z : rows - z], last], axis=0)


def sinh_cosh(p):
    a, b = jnp.exp(p - LN2), jnp.exp(-p - LN2)
    q = jnp.minimum(p * p, 1.0)
    small = p * (
        1.0
        + q * (1 / 6) * (1.0 + q * (1 / 20) * (1.0 + q * (1 / 42) * (1.0 + q * (1 / 72) * (1.0 + q * (1 / 110)))))
    )
    return jnp.where(jnp.abs(p) < 1.0, small, a - b), a + b


def taper_y(density):
    width = density.shape[1]
    lane = iota(density.shape, 1)
    summed = float(taper_weights[4]) * density
    for k in range(1, 5):
        before = jnp.where(lane < k, 0.0, pltpu.roll(density, k, 1))
        after = jnp.where(lane >= width - k, 0.0, pltpu.roll(density, width - k, 1))
        summed = summed + float(taper_weights[4 + k]) * (before + after)
    return summed


def taper_z(rows, z, cx):
    i, j = iota((rows, rows), 0), iota((rows, rows), 1)
    far = jnp.abs((i & (z - 1)) - (j >> log2(cx)))
    band = jnp.zeros((rows, rows), jnp.float32)
    for k in range(5):
        band = jnp.where(far == k, float(taper_weights[4 + k]), band)
    return jnp.where((i >> log2(z)) == (j & (cx - 1)), band, 0.0)


def scattered(cells, values, rows, z, cx, y):
    entries = cells.shape[1]
    ly, lx = log2(y), log2(cx)
    row = ((cells >> ly) & (cx - 1)) * z + (cells >> (ly + lx))
    at_row = jnp.where(iota((rows, entries), 0) == row, values, 0.0)
    at_y = jnp.where(iota((y, entries), 0) == (cells & (y - 1)), jnp.float32(1.0), jnp.float32(0.0))
    return lax.dot_general(
        at_row, at_y, (((1,), (1,)), ((), ())),
        precision=lax.Precision.HIGHEST, preferred_element_type=jnp.float32,
    )


def solver(
    slabs, bulks, nz, cx, y,
    atoms_hbm, flags_hbm, cells_hbm, values_hbm, pot_ref, mis_ref,
    atoms_in, flags_in, cells_in, values_in,
    ay, abuf, ty, hty,
    w0, w1, w2, w3, v2_ref,
    sx0, hx0, sy0, hy0, sx1, hx1, sy1, hy1,
    own, buf1, buf2,
    send_sem, recv_sem, s1_send, s1_recv, s2_send, s2_recv,
    a_send, a_recv, t_send, t_recv, load_sem,
):
    s, b = lax.axis_index("slab"), lax.axis_index("bulk")
    z0, z1, z2, z3 = nz, nz // 2, nz // 4, nz // 8
    rows0, rows1 = cx * z0, (cx // 2) * z1
    r2 = (cx // 4) * z2
    y1 = y // 2
    y2 = y // 4
    loads = [
        pltpu.make_async_copy(there, here, load_sem.at[i])
        for i, (there, here) in enumerate((
            (atoms_hbm, atoms_in), (flags_hbm, flags_in),
            (cells_hbm, cells_in), (values_hbm, values_in),
        ))
    ]
    for load in loads:
        load.start()
    for ref in (hx0, hy0, hx1, hy1, hty):
        ref[...] = jnp.zeros_like(ref)

    count = slabs * bulks
    me = s * bulks + b
    barrier = pltpu.get_barrier_semaphore()

    for k in range(1, slabs):
        pl.semaphore_signal(
            barrier, inc=1, device_id=(lax.rem(s + k, slabs), b), device_id_type=MESH_ID
        )
    for k in range(1, bulks):
        pl.semaphore_signal(
            barrier, inc=1, device_id=(s, lax.rem(b + k, bulks)), device_id_type=MESH_ID
        )

    def halo_copies(level, phase):
        sx, hx, sy, hy = (sx0, hx0, sy0, hy0) if level == 0 else (sx1, hx1, sy1, hy1)
        slot = phase if level == 0 else 7 + phase
        made = []
        for side, (src, dst, to, can_send, can_recv) in enumerate((
            (sx.at[phase, 0], hx.at[phase, 0], (s, b + 1), b < bulks - 1, b > 0),
            (sx.at[phase, 1], hx.at[phase, 1], (s, b - 1), b > 0, b < bulks - 1),
            (sy.at[phase, 0], hy.at[phase, 0], (s + 1, b), s < slabs - 1, s > 0),
            (sy.at[phase, 1], hy.at[phase, 1], (s - 1, b), s > 0, s < slabs - 1),
        )):
            copy = pltpu.make_async_remote_copy(
                src_ref=src, dst_ref=dst,
                send_sem=send_sem.at[slot, side], recv_sem=recv_sem.at[slot, side],
                device_id=to, device_id_type=MESH_ID,
            )
            made.append((copy, can_send, can_recv))
        return made

    def start(level, phase, v):
        sx, sy = (sx0, sy0) if level == 0 else (sx1, sy1)
        z = z0 if level == 0 else z1
        rows, ys = v.shape
        sx[phase, 0] = v[rows - z :]
        sx[phase, 1] = v[:z]
        lane = iota((8, 128), 1)
        for side, at in ((0, ys - 1), (1, 0)):
            packed = jnp.zeros((8, 128), jnp.float32)
            for k in range(rows // 8):
                column = jnp.broadcast_to(v[8 * k : 8 * k + 8, at : at + 1], (8, 128))
                packed = jnp.where(lane == k, column, packed)
            sy[phase, side] = packed
        for copy, can_send, _ in halo_copies(level, phase):
            pl.when(can_send)(copy.start)

    def finish(level, phase):
        hx, hy = (hx0, hy0) if level == 0 else (hx1, hy1)
        rows, ys = (rows0, y) if level == 0 else (rows1, y1)
        for copy, _, can_recv in halo_copies(level, phase):
            pl.when(can_recv)(copy.wait_recv)
        low, high = hy[phase, 0], hy[phase, 1]
        lane = iota((8, ys), 1)
        tiles = []
        for k in range(rows // 8):
            tiles.append(jnp.where(
                lane == 0,
                jnp.broadcast_to(low[:, k : k + 1], (8, ys)),
                jnp.broadcast_to(high[:, k : k + 1], (8, ys)),
            ))
        return hx[phase, 0], hx[phase, 1], jnp.concatenate(tiles, axis=0)

    def around(level, phase, w_ref, v, z):
        start(level, phase, v)
        inner = laplace(w_ref, v, z, NO_HALO)
        return rim_part(w_ref, inner, z, finish(level, phase))

    def gather_copies(n, stage):
        made = []
        size, me = (slabs, s) if stage == 0 else (bulks, b)
        for k in range(1, size):
            to = lax.rem(me + k, size)
            came = lax.rem(me + size - k, size)
            if stage == 0:
                make = lambda slot: pltpu.make_async_remote_copy(
                    src_ref=own.at[n], dst_ref=buf1.at[n, slot],
                    send_sem=s1_send.at[n, k], recv_sem=s1_recv.at[n, k],
                    device_id=(to, b), device_id_type=MESH_ID,
                )
            else:
                make = lambda slot: pltpu.make_async_remote_copy(
                    src_ref=buf1.at[n], dst_ref=buf2.at[n, slot],
                    send_sem=s2_send.at[n, k], recv_sem=s2_recv.at[n, k],
                    device_id=(s, to), device_id_type=MESH_ID,
                )
            made.append((make(me), make(came)))
        return made

    def gather_begin(n, message):
        own[n] = message
        for out, _ in gather_copies(n, 0):
            out.start()
        buf1[n, s] = message

    def gather_pass(n):
        for _, into in gather_copies(n, 0):
            into.wait_recv()
        for out, _ in gather_copies(n, 1):
            out.start()
        buf2[n, b] = buf1[n]

    def gather_end(n):
        for _, into in gather_copies(n, 1):
            into.wait_recv()

    def take(n, half):
        lane = iota((bulks * r2, 128), 1)
        tiles = []
        for t in range(slabs // 2):
            lo = buf2[n, :, 2 * t].reshape(bulks * r2, 128)
            hi = buf2[n, :, 2 * t + 1].reshape(bulks * r2, 128)
            if half == 0:
                hi = pltpu.roll(hi, 64, 1)
            else:
                lo = pltpu.roll(lo, 64, 1)
            tiles.append(jnp.where(lane < 64, lo, hi))
        return jnp.concatenate(tiles, axis=1)

    left12 = left_coarse(rows1, z1)
    right12a = pick((y1, 128), lambda i, j: (i >> 1) == j, 0.5)
    right12b = pick((y1, 128), lambda i, j: (i >> 1) + 64 == j, 0.5)

    loads[0].wait()
    density = atoms_in[...].astype(jnp.float32).reshape(-1, slabs * y)
    smooth_y = taper_y(density)
    for t in range(slabs):
        ay[t] = smooth_y[:, t * y : (t + 1) * y]
    slab_copies = []
    for k in range(1, slabs):
        to, came = lax.rem(s + k, slabs), lax.rem(s + slabs - k, slabs)
        slab_copies.append([
            pltpu.make_async_remote_copy(
                src_ref=ay.at[to], dst_ref=abuf.at[slot],
                send_sem=a_send.at[k], recv_sem=a_recv.at[k],
                device_id=(to, b), device_id_type=MESH_ID,
            )
            for slot in (s, came)
        ])
    pl.semaphore_wait(barrier, slabs + bulks - 2)
    for out, _ in slab_copies:
        out.start()
    abuf[s] = ay[s]
    for load in loads[1:]:
        load.wait()
    src = scattered(cells_in[...], values_in[...], rows0, z0, cx, y)
    to_x = pick((rows0, rows0), lambda i, j: (i >> log2(z0)) + ((i & (z0 - 1)) << log2(cx)) == j, 1.0)
    open_cells = 1.0 - mm(to_x, flags_in[...].astype(jnp.float32).reshape(rows0, y))
    along_z = taper_z(rows0, z0, cx)
    for _, into in slab_copies:
        into.wait_recv()
    smooth_z = mm(along_z, abuf[...].reshape(rows0, y))
    ty[0] = smooth_z[rows0 - 4 * z0 :]
    ty[1] = smooth_z[: 4 * z0]
    row_copies = []
    for side, (to, can_send, can_recv) in enumerate((
        ((s, b + 1), b < bulks - 1, b > 0),
        ((s, b - 1), b > 0, b < bulks - 1),
    )):
        row_copies.append((
            pltpu.make_async_remote_copy(
                src_ref=ty.at[side], dst_ref=hty.at[side],
                send_sem=t_send.at[side], recv_sem=t_recv.at[side],
                device_id=to, device_id_type=MESH_ID,
            ), can_send, can_recv,
        ))
    for copy, can_send, _ in row_copies:
        pl.when(can_send)(copy.start)
    for copy, _, can_recv in row_copies:
        pl.when(can_recv)(copy.wait_recv)
    extended = jnp.concatenate([hty[0], smooth_z, hty[1]], axis=0)
    smoothed = float(taper_weights[0]) * extended[:rows0]
    for k in range(1, 9):
        smoothed = smoothed + float(taper_weights[k]) * extended[k * z0 : k * z0 + rows0]
    shading = jnp.exp(-smoothed / density_scale)
    d0 = 2.0 + 78.0 * shading
    rb = screening * shading * shading * open_cells
    start(0, 0, d0)
    d1 = coarse2(d0, z0)
    start(1, 0, d1)
    gather_begin(NEWTON, mm(left12, mm(d1, right12a)))
    face0 = put_weights(w0, d0, z0, finish(0, 0), 1.0)
    face1 = put_weights(w1, d1, z1, finish(1, 0), 0.25)
    gather_pass(NEWTON)
    face2 = face3 = None
    pot = None
    for n in range(NEWTON):
        if n == 0:
            target, c0 = src, rb
        else:
            sh, ch = sinh_cosh(pot)
            target = src - around(0, 3 * n, w0, pot, z0) - rb * sh
            c0 = rb * ch
        step0 = damping / (face0 + c0)
        v0 = step0 * target
        start(0, 3 * n + 1, v0)
        c1 = coarse2(c0, z0)
        step1 = damping / (face1 + c1)
        inner0 = laplace(w0, v0, z0, NO_HALO)
        res0 = target - rim_part(w0, inner0, z0, finish(0, 3 * n + 1)) - c0 * v0
        t1 = coarse2(res0, z0)
        v1 = step1 * t1
        start(1, n + 1, v1)
        inner1 = laplace(w1, v1, z1, NO_HALO)
        c1_part = mm(c1, right12b)
        xlo1, xhi1, edge1 = finish(1, n + 1)
        res1 = t1 - rim_part(w1, inner1, z1, (xlo1, xhi1, edge1)) - c1 * v1
        message = mm(left12, mm(res1, right12a) + c1_part)
        gather_begin(n, message)
        gather_pass(n)
        gather_end(n)
        t2, c2 = take(n, 0), take(n, 1)
        if n == 0:
            gather_end(NEWTON)
            d2 = take(NEWTON, 0)
            d3 = coarse2(d2, z2)
            face2 = put_weights(w2, d2, z2, NO_HALO, 0.25**2)
            face3 = put_weights(w3, d3, z3, NO_HALO, 0.25**3)
        step2 = damping / (face2 + c2)
        v2 = step2 * t2
        res2 = t2 - laplace(w2, v2, z2, NO_HALO) - c2 * v2
        t3, c3 = coarse2(res2, z2), coarse2(c2, z2)
        step3 = damping / (face3 + c3)
        v3 = step3 * t3
        for repeat in range(COARSE - 1):
            v3 = v3 + step3 * (t3 - laplace(w3, v3, z3, NO_HALO) - c3 * v3)
        v2 = v2 + fine2(v3, z2)
        v2 = v2 + step2 * (t2 - laplace(w2, v2, z2, NO_HALO) - c2 * v2)
        v2_ref[0:r2] = jnp.zeros((r2, slabs * y2), jnp.float32)
        v2_ref[r2 : r2 + bulks * r2] = v2
        v2_ref[r2 + bulks * r2 :] = jnp.zeros((r2, slabs * y2), jnp.float32)
        near = v2_ref[pl.ds(pl.multiple_of(b * r2, 8), 3 * r2), :]
        mine = pick((slabs * y2, y1), lambda i, j: i == (j >> 1) + s * y2, 1.0)
        rims = pick(
            (slabs * y2, y1),
            lambda i, j: ((j == 0) & (i == s * y2 - 1)) | ((j == y1 - 1) & (i == s * y2 + y2)),
            1.0,
        )
        near_mine = mm(near, mine)
        up = left_fine(rows1, z1)
        v1 = v1 + mm(up, near_mine[r2 : 2 * r2])
        xlo1 = xlo1 + mm(up, near_mine[0:r2])[rows1 - z1 :]
        xhi1 = xhi1 + mm(up, near_mine[2 * r2 :])[:z1]
        edge1 = edge1 + mm(up, mm(near[r2 : 2 * r2], rims))
        v1 = v1 + step1 * (t1 - laplace(w1, v1, z1, (xlo1, xhi1, edge1)) - c1 * v1)
        v0 = v0 + fine2(v1, z0)
        v0 = v0 + step0 * (target - around(0, 3 * n + 2, w0, v0, z0) - c0 * v0)
        pot = v0 if n == 0 else pot + v0
    start(0, 3 * NEWTON, pot)
    from_x = pick((rows0, rows0), lambda i, j: (j >> log2(z0)) + ((j & (z0 - 1)) << log2(cx)) == i, 1.0)
    pot_ref[...] = mm(from_x, pot).reshape(nz, cx, y)
    sh, _ = sinh_cosh(pot)
    inner = laplace(w0, pot, z0, NO_HALO) + rb * sh - src
    misfit = rim_part(w0, inner, z0, finish(0, 3 * NEWTON))
    mis_ref[...] = mm(from_x, misfit).reshape(nz, cx, y)

    for out, _ in slab_copies:
        out.wait_send()
    for copy, can_send, _ in row_copies:
        pl.when(can_send)(copy.wait_send)
    for level, count in ((0, 7), (1, 3)):
        for phase in range(count):
            for copy, can_send, _ in halo_copies(level, phase):
                pl.when(can_send)(copy.wait_send)
    for n in range(NEWTON + 1):
        for stage in range(2):
            for out, _ in gather_copies(n, stage):
                out.wait_send()


def per_device(atom_counts, ion_flags, charge_cells, charge_values):
    slabs, bulks = lax.axis_size("slab"), lax.axis_size("bulk")
    nz, cx, y = ion_flags.shape
    rows = nz * cx
    rows2 = (cx // 4) * (nz // 4)
    f32 = jnp.float32
    whole2 = (bulks * rows2, slabs * (y // 4))
    vm = pltpu.VMEM
    pot, mis = pl.pallas_call(
        lambda *refs: solver(slabs, bulks, nz, cx, y, *refs),
        out_shape=[jax.ShapeDtypeStruct((nz, cx, y), f32)] * 2,
        in_specs=[pl.BlockSpec(memory_space=pl.ANY)] * 4,
        out_specs=[pl.BlockSpec(memory_space=pltpu.VMEM)] * 2,
        scratch_shapes=[
            vm(atom_counts.shape, jnp.int32), vm(ion_flags.shape, jnp.int32),
            vm((1,) + charge_cells.shape, jnp.int32), vm((1,) + charge_values.shape, f32),
            vm((slabs, rows // slabs, y), f32), vm((slabs, rows // slabs, y), f32),
            vm((2, 4 * nz, y), f32), vm((2, 4 * nz, y), f32),
            vm((6, rows, y), f32),
            vm((6, rows // 4, y // 2), f32),
            vm((6,) + whole2, f32),
            vm((6, whole2[0] // 4, whole2[1] // 2), f32),
            vm((whole2[0] + 2 * rows2, whole2[1]), f32),
            vm((7, 2, nz, y), f32), vm((7, 2, nz, y), f32),
            vm((7, 2, 8, 128), f32), vm((7, 2, 8, 128), f32),
            vm((3, 2, nz // 2, y // 2), f32), vm((3, 2, nz // 2, y // 2), f32),
            vm((3, 2, 8, 128), f32), vm((3, 2, 8, 128), f32),
            vm((NEWTON + 1, rows2, 128), f32),
            vm((NEWTON + 1, slabs, rows2, 128), f32),
            vm((NEWTON + 1, bulks, slabs, rows2, 128), f32),
            pltpu.SemaphoreType.DMA((10, 4)), pltpu.SemaphoreType.DMA((10, 4)),
            pltpu.SemaphoreType.DMA((NEWTON + 1, slabs)), pltpu.SemaphoreType.DMA((NEWTON + 1, slabs)),
            pltpu.SemaphoreType.DMA((NEWTON + 1, bulks)), pltpu.SemaphoreType.DMA((NEWTON + 1, bulks)),
            pltpu.SemaphoreType.DMA((slabs,)), pltpu.SemaphoreType.DMA((slabs,)),
            pltpu.SemaphoreType.DMA((2,)), pltpu.SemaphoreType.DMA((2,)),
            pltpu.SemaphoreType.DMA((4,)),
        ],
        compiler_params=pltpu.CompilerParams(
            collective_id=0, has_side_effects=True, vmem_limit_bytes=40 << 20
        ),
    )(atom_counts, ion_flags, charge_cells[None], charge_values[None])
    return pot, mis


def solution(mesh):
    placed = (
        P("slab", "bulk", None),
        P(None, "bulk", "slab"),
        P(("slab", "bulk")),
        P(("slab", "bulk")),
    )
    return jax.shard_map(
        per_device,
        mesh=mesh,
        in_specs=placed,
        out_specs=(P(None, "bulk", "slab"), P(None, "bulk", "slab")),
        check_vma=False,
    )
```

```python
import jax
import jax.numpy as jnp
import numpy as np
from jax import lax
from jax.experimental import pallas as pl
from jax.experimental.pallas import tpu as pltpu
from jax.sharding import PartitionSpec as P

GRID_LEVEL_COUNT = 4
COARSE = 8
NEWTON = 2


taper_raw = np.exp(-0.5 * (np.arange(-4, 5) / 1.5) ** 2)
taper_weights = taper_raw / taper_raw.sum()
damping = 0.8
screening = 1.0
density_scale = 2.0


MESH_ID = pl.DeviceIdType.MESH
GATHER_UNROLL = 1
LN2 = float(np.log(2.0))


def iota(shape, dim):
    return lax.broadcasted_iota(jnp.int32, shape, dim)


def log2(n):
    return int(n).bit_length() - 1


def mm(a, b):
    return lax.dot_general(
        a, b, (((1,), (0,)), ((), ())),
        precision=lax.Precision.HIGHEST, preferred_element_type=jnp.float32,
    )


def thirds(v):
    high = v.astype(jnp.bfloat16)
    rest = v - high.astype(jnp.float32)
    middle = rest.astype(jnp.bfloat16)
    return high, middle, (rest - middle.astype(jnp.float32)).astype(jnp.bfloat16)


def dot16(a, b):
    return lax.dot_general(a, b, (((1,), (0,)), ((), ())), preferred_element_type=jnp.float32)


def left_mm(a, v):
    a = a.astype(jnp.bfloat16)
    high, middle, low = [dot16(a, part) for part in thirds(v)]
    return high + (middle + low)


def right_mm(v, b):
    b = b.astype(jnp.bfloat16)
    high, middle, low = [dot16(part, b) for part in thirds(v)]
    return high + (middle + low)


def pick(shape, test, value):
    return jnp.where(test(iota(shape, 0), iota(shape, 1)), jnp.float32(value), jnp.float32(0.0))


def left_coarse(rows, z):
    lz = log2(z)

    def test(i, j):
        return ((i >> (lz - 1)) == (j >> (lz + 1))) & (
            (i & (z // 2 - 1)) == ((j & (z - 1)) >> 1)
        )

    return pick((rows // 4, rows), test, 0.25)


def left_fine(rows, z):
    lz = log2(z)

    def test(j, i):
        return ((i >> (lz - 1)) == (j >> (lz + 1))) & (
            (i & (z // 2 - 1)) == ((j & (z - 1)) >> 1)
        )

    return pick((rows, rows // 4), test, 1.0)


def right_coarse(y):
    return pick((y, y // 2), lambda i, j: (i >> 1) == j, 0.5)


def right_fine(y):
    return pick((y // 2, y), lambda i, j: i == (j >> 1), 1.0)


def coarse2(v, z):
    return right_mm(left_mm(left_coarse(v.shape[0], z), v), right_coarse(v.shape[1]))


def fine2(v, z):
    return left_mm(left_fine(v.shape[0] * 4, z), right_mm(v, right_fine(v.shape[1] * 2)))


def neighbours(v, z, xlo, xhi, edge):
    rows, y = v.shape
    row, lane = iota(v.shape, 0), iota(v.shape, 1)
    if xlo is None:
        xm = jnp.where(row < z, 0.0, pltpu.roll(v, z, 0))
        xp = jnp.where(row >= rows - z, 0.0, pltpu.roll(v, rows - z, 0))
        edge = jnp.zeros_like(v)
    else:
        xm = jnp.concatenate([xlo, v[: rows - z]], axis=0)
        xp = jnp.concatenate([v[z:], xhi], axis=0)
    zrow = row & (z - 1)
    zm = jnp.where(zrow == 0, 0.0, pltpu.roll(v, 1, 0))
    zp = jnp.where(zrow == z - 1, 0.0, pltpu.roll(v, rows - 1, 0))
    ym = jnp.where(lane == 0, edge, pltpu.roll(v, 1, 1))
    yp = jnp.where(lane == y - 1, edge, pltpu.roll(v, y - 1, 1))
    return xm, xp, zm, zp, ym, yp


def put_weights(w_ref, d, z, halo, scaling):
    total = None
    for i, other in enumerate(neighbours(d, z, *halo)):
        w = (0.5 * scaling) * (d + other)
        w_ref[i] = w
        total = w if total is None else total + w
    return total


def laplace(w_ref, v, z, halo):
    total = None
    for i, other in enumerate(neighbours(v, z, *halo)):
        term = w_ref[i] * (v - other)
        total = term if total is None else total + term
    return total


NO_HALO = (None, None, None)


def rim_part(w_ref, inner, z, halo):
    xlo, xhi, edge = halo
    rows, y = inner.shape
    lane = iota(inner.shape, 1)
    inner = inner - jnp.where(lane == 0, w_ref[4] * edge, jnp.where(lane == y - 1, w_ref[5] * edge, 0.0))
    first = inner[:z] - w_ref[0, :z] * xlo
    last = inner[rows - z :] - w_ref[1, rows - z :] * xhi
    return jnp.concatenate([first, inner[z : rows - z], last], axis=0)


def sinh_cosh(p):
    a, b = jnp.exp(p - LN2), jnp.exp(-p - LN2)
    q = jnp.minimum(p * p, 1.0)
    small = p * (
        1.0
        + q * (1 / 6) * (1.0 + q * (1 / 20) * (1.0 + q * (1 / 42) * (1.0 + q * (1 / 72) * (1.0 + q * (1 / 110)))))
    )
    return jnp.where(jnp.abs(p) < 1.0, small, a - b), a + b


def taper_y(density):
    width = density.shape[1]
    lane = iota(density.shape, 1)
    summed = float(taper_weights[4]) * density
    for k in range(1, 5):
        before = jnp.where(lane < k, 0.0, pltpu.roll(density, k, 1))
        after = jnp.where(lane >= width - k, 0.0, pltpu.roll(density, width - k, 1))
        summed = summed + float(taper_weights[4 + k]) * (before + after)
    return summed


def taper_z(rows, z, cx):
    i, j = iota((rows, rows), 0), iota((rows, rows), 1)
    far = jnp.abs((i & (z - 1)) - (j >> log2(cx)))
    band = jnp.zeros((rows, rows), jnp.float32)
    for k in range(5):
        band = jnp.where(far == k, float(taper_weights[4 + k]), band)
    return jnp.where((i >> log2(z)) == (j & (cx - 1)), band, 0.0)


def scattered(cells, values, rows, z, cx, y):
    entries = cells.shape[1]
    ly, lx = log2(y), log2(cx)
    row = ((cells >> ly) & (cx - 1)) * z + (cells >> (ly + lx))
    at_row = jnp.where(iota((rows, entries), 0) == row, values, 0.0)
    at_y = jnp.where(iota((y, entries), 0) == (cells & (y - 1)), jnp.float32(1.0), jnp.float32(0.0))
    return lax.dot_general(
        at_row, at_y, (((1,), (1,)), ((), ())),
        precision=lax.Precision.HIGHEST, preferred_element_type=jnp.float32,
    )


def solver(
    slabs, bulks, nz, cx, y,
    atoms_hbm, flags_hbm, cells_hbm, values_hbm, pot_ref, mis_ref,
    atoms_in, flags_in, cells_in, values_in,
    ay, abuf, ty, hty,
    w0, w1, w2, w3, v2_ref,
    sx0, hx0, sy0, hy0, sx1, hx1, sy1, hy1,
    own, buf1, buf2,
    send_sem, recv_sem, s1_send, s1_recv, s2_send, s2_recv,
    a_send, a_recv, t_send, t_recv, load_sem,
):
    s, b = lax.axis_index("slab"), lax.axis_index("bulk")
    z0, z1, z2, z3 = nz, nz // 2, nz // 4, nz // 8
    rows0, rows1 = cx * z0, (cx // 2) * z1
    r2 = (cx // 4) * z2
    y1 = y // 2
    y2 = y // 4
    loads = [
        pltpu.make_async_copy(there, here, load_sem.at[i])
        for i, (there, here) in enumerate((
            (atoms_hbm, atoms_in), (flags_hbm, flags_in),
            (cells_hbm, cells_in), (values_hbm, values_in),
        ))
    ]
    for load in loads:
        load.start()
    for ref in (hx0, hy0, hx1, hy1, hty):
        ref[...] = jnp.zeros_like(ref)

    count = slabs * bulks
    me = s * bulks + b
    barrier = pltpu.get_barrier_semaphore()

    for k in range(1, slabs):
        pl.semaphore_signal(
            barrier, inc=1, device_id=(lax.rem(s + k, slabs), b), device_id_type=MESH_ID
        )
    for k in range(1, bulks):
        pl.semaphore_signal(
            barrier, inc=1, device_id=(s, lax.rem(b + k, bulks)), device_id_type=MESH_ID
        )

    def halo_copies(level, phase):
        sx, hx, sy, hy = (sx0, hx0, sy0, hy0) if level == 0 else (sx1, hx1, sy1, hy1)
        slot = phase if level == 0 else 7 + phase
        made = []
        for side, (src, dst, to, can_send, can_recv) in enumerate((
            (sx.at[phase, 0], hx.at[phase, 0], (s, b + 1), b < bulks - 1, b > 0),
            (sx.at[phase, 1], hx.at[phase, 1], (s, b - 1), b > 0, b < bulks - 1),
            (sy.at[phase, 0], hy.at[phase, 0], (s + 1, b), s < slabs - 1, s > 0),
            (sy.at[phase, 1], hy.at[phase, 1], (s - 1, b), s > 0, s < slabs - 1),
        )):
            copy = pltpu.make_async_remote_copy(
                src_ref=src, dst_ref=dst,
                send_sem=send_sem.at[slot, side], recv_sem=recv_sem.at[slot, side],
                device_id=to, device_id_type=MESH_ID,
            )
            made.append((copy, can_send, can_recv))
        return made

    def start(level, phase, v):
        sx, sy = (sx0, sy0) if level == 0 else (sx1, sy1)
        z = z0 if level == 0 else z1
        rows, ys = v.shape
        sx[phase, 0] = v[rows - z :]
        sx[phase, 1] = v[:z]
        copies = halo_copies(level, phase)
        for copy, can_send, _ in copies[:2]:
            pl.when(can_send)(copy.start)
        lane = iota((8, 128), 1)
        for side, at in ((0, ys - 1), (1, 0)):
            packed = jnp.zeros((8, 128), jnp.float32)
            for k in range(rows // 8):
                column = jnp.broadcast_to(v[8 * k : 8 * k + 8, at : at + 1], (8, 128))
                packed = jnp.where(lane == k, column, packed)
            sy[phase, side] = packed
            copy, can_send, _ = copies[2 + side]
            pl.when(can_send)(copy.start)

    def finish(level, phase):
        hx, hy = (hx0, hy0) if level == 0 else (hx1, hy1)
        rows, ys = (rows0, y) if level == 0 else (rows1, y1)
        copies = halo_copies(level, phase)
        for copy, _, can_recv in copies[2:]:
            pl.when(can_recv)(copy.wait_recv)
        low, high = hy[phase, 0], hy[phase, 1]
        lane = iota((8, ys), 1)
        tiles = []
        for k in range(rows // 8):
            tiles.append(jnp.where(
                lane == 0,
                jnp.broadcast_to(low[:, k : k + 1], (8, ys)),
                jnp.broadcast_to(high[:, k : k + 1], (8, ys)),
            ))
        edge = jnp.concatenate(tiles, axis=0)
        for copy, _, can_recv in copies[:2]:
            pl.when(can_recv)(copy.wait_recv)
        return hx[phase, 0], hx[phase, 1], edge

    def around(level, phase, w_ref, v, z):
        start(level, phase, v)
        inner = laplace(w_ref, v, z, NO_HALO)
        return rim_part(w_ref, inner, z, finish(level, phase))

    def gather_copies(n, stage):
        made = []
        size, me = (slabs, s) if stage == 0 else (bulks, b)
        for k in range(1, size):
            to = lax.rem(me + k, size)
            came = lax.rem(me + size - k, size)
            if stage == 0:
                make = lambda slot: pltpu.make_async_remote_copy(
                    src_ref=own.at[n], dst_ref=buf1.at[n, slot],
                    send_sem=s1_send.at[n, k], recv_sem=s1_recv.at[n, k],
                    device_id=(to, b), device_id_type=MESH_ID,
                )
            else:
                make = lambda slot: pltpu.make_async_remote_copy(
                    src_ref=buf1.at[n], dst_ref=buf2.at[n, slot],
                    send_sem=s2_send.at[n, k], recv_sem=s2_recv.at[n, k],
                    device_id=(s, to), device_id_type=MESH_ID,
                )
            made.append((make(me), make(came)))
        return made

    def gather_begin(n, message):
        own[n] = message
        for out, _ in gather_copies(n, 0):
            out.start()
        buf1[n, s] = message

    def gather_pass(n):
        for _, into in gather_copies(n, 0):
            into.wait_recv()
        for out, _ in gather_copies(n, 1):
            out.start()
        buf2[n, b] = buf1[n]

    def gather_end(n):
        for _, into in gather_copies(n, 1):
            into.wait_recv()

    def take(n, half):
        lane = iota((bulks * r2, 128), 1)
        tiles = []
        for t in range(slabs // 2):
            lo = buf2[n, :, 2 * t].reshape(bulks * r2, 128)
            hi = buf2[n, :, 2 * t + 1].reshape(bulks * r2, 128)
            if half == 0:
                hi = pltpu.roll(hi, 64, 1)
            else:
                lo = pltpu.roll(lo, 64, 1)
            tiles.append(jnp.where(lane < 64, lo, hi))
        return jnp.concatenate(tiles, axis=1)

    left12 = left_coarse(rows1, z1)
    right12a = pick((y1, 128), lambda i, j: (i >> 1) == j, 0.5)
    right12b = pick((y1, 128), lambda i, j: (i >> 1) + 64 == j, 0.5)

    loads[0].wait()
    density = atoms_in[...].astype(jnp.float32).reshape(-1, slabs * y)
    smooth_y = taper_y(density)
    for t in range(slabs):
        ay[t] = smooth_y[:, t * y : (t + 1) * y]
    slab_copies = []
    for k in range(1, slabs):
        to, came = lax.rem(s + k, slabs), lax.rem(s + slabs - k, slabs)
        slab_copies.append([
            pltpu.make_async_remote_copy(
                src_ref=ay.at[to], dst_ref=abuf.at[slot],
                send_sem=a_send.at[k], recv_sem=a_recv.at[k],
                device_id=(to, b), device_id_type=MESH_ID,
            )
            for slot in (s, came)
        ])
    pl.semaphore_wait(barrier, slabs + bulks - 2)
    for out, _ in slab_copies:
        out.start()
    abuf[s] = ay[s]
    for load in loads[1:]:
        load.wait()
    src = scattered(cells_in[...], values_in[...], rows0, z0, cx, y)
    to_x = pick((rows0, rows0), lambda i, j: (i >> log2(z0)) + ((i & (z0 - 1)) << log2(cx)) == j, 1.0)
    open_cells = 1.0 - left_mm(to_x, flags_in[...].astype(jnp.float32).reshape(rows0, y))
    along_z = taper_z(rows0, z0, cx)
    for _, into in slab_copies:
        into.wait_recv()
    smooth_z = mm(along_z, abuf[...].reshape(rows0, y))
    ty[0] = smooth_z[rows0 - 4 * z0 :]
    ty[1] = smooth_z[: 4 * z0]
    row_copies = []
    for side, (to, can_send, can_recv) in enumerate((
        ((s, b + 1), b < bulks - 1, b > 0),
        ((s, b - 1), b > 0, b < bulks - 1),
    )):
        row_copies.append((
            pltpu.make_async_remote_copy(
                src_ref=ty.at[side], dst_ref=hty.at[side],
                send_sem=t_send.at[side], recv_sem=t_recv.at[side],
                device_id=to, device_id_type=MESH_ID,
            ), can_send, can_recv,
        ))
    for copy, can_send, _ in row_copies:
        pl.when(can_send)(copy.start)
    for copy, _, can_recv in row_copies:
        pl.when(can_recv)(copy.wait_recv)
    extended = jnp.concatenate([hty[0], smooth_z, hty[1]], axis=0)
    smoothed = float(taper_weights[0]) * extended[:rows0]
    for k in range(1, 9):
        smoothed = smoothed + float(taper_weights[k]) * extended[k * z0 : k * z0 + rows0]
    shading = jnp.exp(-smoothed / density_scale)
    d0 = 2.0 + 78.0 * shading
    rb = screening * shading * shading * open_cells
    start(0, 0, d0)
    d1 = coarse2(d0, z0)
    start(1, 0, d1)
    gather_begin(NEWTON, left_mm(left12, right_mm(d1, right12a)))
    face0 = put_weights(w0, d0, z0, finish(0, 0), 1.0)
    face1 = put_weights(w1, d1, z1, finish(1, 0), 0.25)
    gather_pass(NEWTON)
    face2 = face3 = None
    pot = None
    for n in range(NEWTON):
        if n == 0:
            target, c0 = src, rb
        else:
            sh, ch = sinh_cosh(pot)
            target = src - around(0, 3 * n, w0, pot, z0) - rb * sh
            c0 = rb * ch
        step0 = damping / (face0 + c0)
        v0 = step0 * target
        start(0, 3 * n + 1, v0)
        c1 = coarse2(c0, z0)
        step1 = damping / (face1 + c1)
        inner0 = laplace(w0, v0, z0, NO_HALO)
        res0 = target - rim_part(w0, inner0, z0, finish(0, 3 * n + 1)) - c0 * v0
        t1 = coarse2(res0, z0)
        v1 = step1 * t1
        start(1, n + 1, v1)
        inner1 = laplace(w1, v1, z1, NO_HALO)
        c1_part = right_mm(c1, right12b)
        xlo1, xhi1, edge1 = finish(1, n + 1)
        res1 = t1 - rim_part(w1, inner1, z1, (xlo1, xhi1, edge1)) - c1 * v1
        message = left_mm(left12, right_mm(res1, right12a) + c1_part)
        gather_begin(n, message)
        gather_pass(n)
        gather_end(n)
        t2, c2 = take(n, 0), take(n, 1)
        if n == 0:
            gather_end(NEWTON)
            d2 = take(NEWTON, 0)
            d3 = coarse2(d2, z2)
            face2 = put_weights(w2, d2, z2, NO_HALO, 0.25**2)
            face3 = put_weights(w3, d3, z3, NO_HALO, 0.25**3)
        step2 = damping / (face2 + c2)
        v2 = step2 * t2
        res2 = t2 - laplace(w2, v2, z2, NO_HALO) - c2 * v2
        t3, c3 = coarse2(res2, z2), coarse2(c2, z2)
        step3 = damping / (face3 + c3)
        v3 = step3 * t3
        for repeat in range(COARSE - 1):
            v3 = v3 + step3 * (t3 - laplace(w3, v3, z3, NO_HALO) - c3 * v3)
        v2 = v2 + fine2(v3, z2)
        v2 = v2 + step2 * (t2 - laplace(w2, v2, z2, NO_HALO) - c2 * v2)
        v2_ref[0:r2] = jnp.zeros((r2, slabs * y2), jnp.float32)
        v2_ref[r2 : r2 + bulks * r2] = v2
        v2_ref[r2 + bulks * r2 :] = jnp.zeros((r2, slabs * y2), jnp.float32)
        near = v2_ref[pl.ds(pl.multiple_of(b * r2, 8), 3 * r2), :]
        mine = pick((slabs * y2, y1), lambda i, j: i == (j >> 1) + s * y2, 1.0)
        rims = pick(
            (slabs * y2, y1),
            lambda i, j: ((j == 0) & (i == s * y2 - 1)) | ((j == y1 - 1) & (i == s * y2 + y2)),
            1.0,
        )
        near_mine = right_mm(near, mine)
        up = left_fine(rows1, z1)
        v1 = v1 + left_mm(up, near_mine[r2 : 2 * r2])
        xlo1 = xlo1 + left_mm(up, near_mine[0:r2])[rows1 - z1 :]
        xhi1 = xhi1 + left_mm(up, near_mine[2 * r2 :])[:z1]
        edge1 = edge1 + left_mm(up, right_mm(near[r2 : 2 * r2], rims))
        v1 = v1 + step1 * (t1 - laplace(w1, v1, z1, (xlo1, xhi1, edge1)) - c1 * v1)
        v0 = v0 + fine2(v1, z0)
        v0 = v0 + step0 * (target - around(0, 3 * n + 2, w0, v0, z0) - c0 * v0)
        pot = v0 if n == 0 else pot + v0
    start(0, 3 * NEWTON, pot)
    from_x = pick((rows0, rows0), lambda i, j: (j >> log2(z0)) + ((j & (z0 - 1)) << log2(cx)) == i, 1.0)
    pot_ref[...] = left_mm(from_x, pot).reshape(nz, cx, y)
    sh, _ = sinh_cosh(pot)
    inner = laplace(w0, pot, z0, NO_HALO) + rb * sh - src
    misfit = rim_part(w0, inner, z0, finish(0, 3 * NEWTON))
    mis_ref[...] = left_mm(from_x, misfit).reshape(nz, cx, y)

    for out, _ in slab_copies:
        out.wait_send()
    for copy, can_send, _ in row_copies:
        pl.when(can_send)(copy.wait_send)
    for level, count in ((0, 7), (1, 3)):
        for phase in range(count):
            for copy, can_send, _ in halo_copies(level, phase):
                pl.when(can_send)(copy.wait_send)
    for n in range(NEWTON + 1):
        for stage in range(2):
            for out, _ in gather_copies(n, stage):
                out.wait_send()


def per_device(atom_counts, ion_flags, charge_cells, charge_values):
    slabs, bulks = lax.axis_size("slab"), lax.axis_size("bulk")
    nz, cx, y = ion_flags.shape
    rows = nz * cx
    rows2 = (cx // 4) * (nz // 4)
    f32 = jnp.float32
    whole2 = (bulks * rows2, slabs * (y // 4))
    vm = pltpu.VMEM
    pot, mis = pl.pallas_call(
        lambda *refs: solver(slabs, bulks, nz, cx, y, *refs),
        out_shape=[jax.ShapeDtypeStruct((nz, cx, y), f32)] * 2,
        in_specs=[pl.BlockSpec(memory_space=pl.ANY)] * 4,
        out_specs=[pl.BlockSpec(memory_space=pltpu.VMEM)] * 2,
        scratch_shapes=[
            vm(atom_counts.shape, jnp.int32), vm(ion_flags.shape, jnp.int32),
            vm((1,) + charge_cells.shape, jnp.int32), vm((1,) + charge_values.shape, f32),
            vm((slabs, rows // slabs, y), f32), vm((slabs, rows // slabs, y), f32),
            vm((2, 4 * nz, y), f32), vm((2, 4 * nz, y), f32),
            vm((6, rows, y), f32),
            vm((6, rows // 4, y // 2), f32),
            vm((6,) + whole2, f32),
            vm((6, whole2[0] // 4, whole2[1] // 2), f32),
            vm((whole2[0] + 2 * rows2, whole2[1]), f32),
            vm((7, 2, nz, y), f32), vm((7, 2, nz, y), f32),
            vm((7, 2, 8, 128), f32), vm((7, 2, 8, 128), f32),
            vm((3, 2, nz // 2, y // 2), f32), vm((3, 2, nz // 2, y // 2), f32),
            vm((3, 2, 8, 128), f32), vm((3, 2, 8, 128), f32),
            vm((NEWTON + 1, rows2, 128), f32),
            vm((NEWTON + 1, slabs, rows2, 128), f32),
            vm((NEWTON + 1, bulks, slabs, rows2, 128), f32),
            pltpu.SemaphoreType.DMA((10, 4)), pltpu.SemaphoreType.DMA((10, 4)),
            pltpu.SemaphoreType.DMA((NEWTON + 1, slabs)), pltpu.SemaphoreType.DMA((NEWTON + 1, slabs)),
            pltpu.SemaphoreType.DMA((NEWTON + 1, bulks)), pltpu.SemaphoreType.DMA((NEWTON + 1, bulks)),
            pltpu.SemaphoreType.DMA((slabs,)), pltpu.SemaphoreType.DMA((slabs,)),
            pltpu.SemaphoreType.DMA((2,)), pltpu.SemaphoreType.DMA((2,)),
            pltpu.SemaphoreType.DMA((4,)),
        ],
        compiler_params=pltpu.CompilerParams(
            collective_id=0, has_side_effects=True, vmem_limit_bytes=40 << 20
        ),
    )(atom_counts, ion_flags, charge_cells[None], charge_values[None])
    return pot, mis


def solution(mesh):
    placed = (
        P("slab", "bulk", None),
        P(None, "bulk", "slab"),
        P(("slab", "bulk")),
        P(("slab", "bulk")),
    )
    return jax.shard_map(
        per_device,
        mesh=mesh,
        in_specs=placed,
        out_specs=(P(None, "bulk", "slab"), P(None, "bulk", "slab")),
        check_vma=False,
    )
```
